128 devices in a mesh: blk: 32 (over x, z, y_lo), group: 4 (over y_hi, core).
Axes of the slice: x: 4, y: 4 (y_hi: 2, y_lo: 2; y = y_hi * 2 + y_lo), z: 4, core: 2. Of those that a mesh axis runs over, the one named last changes fastest.
Arguments:
- queries: bfloat16 [32, 2048, 2560], P('blk', 'group'), may hold values from -6 to 6
- new_keys: bfloat16 [32, 2048, 256], P('blk', 'group'), may hold values from -15 to 15
- new_values: bfloat16 [32, 2048, 256], P('blk', 'group'), may hold values from -4 to 4
- key_cache: bfloat16 [1280, 128, 256], P('blk', 'group'), may hold values from -4 to 4
- value_cache: bfloat16 [1280, 128, 256], P('blk', 'group'), may hold values from -4 to 4
- out_weight: bfloat16 [2560, 2560], replicated, may hold values from -0.375 to 0.375
- lengths: int32 [32], replicated, may hold values from 0 to 30720, as said below
- page_table: int32 [32, 32], replicated, may hold values from 0 to 1279, as said below
Outputs:
- hidden_states: bfloat16 [32, 2048, 2560], P('blk', 'group')
- key_cache_out: bfloat16 [1280, 128, 256], P('blk', 'group')
- value_cache_out: bfloat16 [1280, 128, 256], P('blk', 'group')
The draws below stay inside these ranges and needn't reach their ends.
Inputs may be any that keep to these rules, and one draw needn't show every extreme that they name: `lengths`: multiples of 2048; some request has length 0 and some has 30720. `page_table`: all entries differ; page p lies on blk index p // 40; columns below 16 hold the request's last 16 pages before its group in order (pages that hold no part of a request where its length is short), the others the pages of its group in order; of one request's first 16 entries at most 1 lie on one blk index, of its last 16 at most 1, and both bounds are reached for every request.
All inputs are finite; a program needn't handle non-finite values.
Results may differ from the reference program's by a relative error of at most 0.009.
Values may be sent and summed in bfloat16 or wider, within the bound.
A program may use at most 256 MiB of HBM per device.

```python
import jax
import jax.numpy as jnp
from jax import lax

D = 2560
HEADS = 10
HD = 256
PAGE = 128
OLD_PAGES = 16
MAX_GROUPS = 16
GROUP = 2048
REQUESTS = 32
WINDOW = 2048
NEW_PAGES = 16
SLOTS = 32
PAGES_DEV = 40
PAGES = 1280


def draw_lengths(key, part):
    counts = jax.random.randint(jax.random.fold_in(key, 11), (REQUESTS,), 0, MAX_GROUPS)
    shuffled = jax.random.permutation(jax.random.fold_in(key, 12), REQUESTS)
    counts = counts.at[shuffled[0]].set(0).at[shuffled[1]].set(MAX_GROUPS - 1)
    return (counts * GROUP).astype(jnp.int32)


def draw_page_table(key, part):
    spread = jax.random.permutation(jax.random.fold_in(key, 21), REQUESTS)
    offset_perm = jax.random.permutation(jax.random.fold_in(key, 22), REQUESTS)
    column = jnp.arange(SLOTS, dtype=jnp.int32)
    owner_of = (spread[column % REQUESTS][None, :] + offset_perm[:, None]) % REQUESTS
    subkeys = jax.random.split(jax.random.fold_in(key, 23), REQUESTS)
    local_perm = jax.vmap(lambda subkey: jax.random.permutation(subkey, PAGES_DEV))(subkeys)
    return (owner_of * PAGES_DEV + local_perm[owner_of, column[None, :]]).astype(jnp.int32)


def draw_queries(key, part):
    array_shape = (REQUESTS, GROUP, HEADS * HD)
    result = 1.5 * jnp.clip(jax.random.normal(jax.random.fold_in(key, 1), array_shape, jnp.float32), -4.0, 4.0)
    return result.astype(jnp.bfloat16)


def draw_new_keys(key, part):
    array_shape = (REQUESTS, GROUP, HD)
    result = jnp.clip(jax.random.normal(jax.random.fold_in(key, 3), array_shape, jnp.float32), -4.0, 4.0)
    return result.astype(jnp.bfloat16)


def level_of(key, shape, shards, smallest, top_value):
    def one(axis_at, parts):
        steps = jax.random.uniform(jax.random.fold_in(jax.random.fold_in(key, 6), axis_at), (parts,), jnp.float32, smallest / len(shards), top_value / len(shards))
        return jnp.repeat(jnp.exp(steps), shape[axis_at] // parts).reshape((-1,) + (1,) * (len(shape) - axis_at - 1))

    level = one(*shards[0])
    for cut in shards[1:]:
        level = level * one(*cut)
    return level


def gaussian(own_key, extent, width, reach, cuts=(), kind=jnp.bfloat16):
    loudness = level_of(own_key, extent, cuts, -0.22, 0.18) if cuts else 1.0
    values = jax.random.normal(own_key, extent, jnp.float32) * width * loudness
    return jnp.minimum(jnp.maximum(values, -reach), reach).astype(kind)


def setup_inputs(seed: int = 0) -> dict:
    arg_keys = jax.random.split(jax.random.key(seed), 9)
    queries = draw_queries(jax.random.fold_in(arg_keys[8], 71), 0)
    new_keys = draw_new_keys(jax.random.fold_in(arg_keys[8], 71), 0)
    new_values = gaussian(arg_keys[2], (REQUESTS, GROUP, HD), 1.0, 4.0, ((0, 32), (1, 4)))
    key_cache = gaussian(arg_keys[3], (PAGES, PAGE, HD), 1.0, 4.0, ((0, 32), (1, 4)))
    value_cache = gaussian(arg_keys[4], (PAGES, PAGE, HD), 1.0, 4.0, ((0, 32), (1, 4)))
    out_weight = gaussian(arg_keys[5], (HEADS * HD, D), HD ** -0.5, 0.375)
    lengths = draw_lengths(jax.random.fold_in(arg_keys[8], 71), 0)
    page_table = draw_page_table(jax.random.fold_in(arg_keys[8], 71), 0)
    return dict(queries=queries, new_keys=new_keys, new_values=new_values, key_cache=key_cache, value_cache=value_cache, out_weight=out_weight, lengths=lengths, page_table=page_table)


masked_score = -1e30


def rotate(values, positions):
    quarter = values.shape[-1] // 4
    freq_table = 10000.0 ** (-jnp.arange(quarter, dtype=jnp.float32) / quarter)
    angles = positions.astype(jnp.float32)[..., None] * freq_table
    cosine = jnp.cos(angles)
    sine_part = jnp.sin(angles)
    leading = values[..., :quarter]
    trailing = values[..., quarter:2 * quarter]
    return jnp.concatenate([leading * cosine - trailing * sine_part, trailing * cosine + leading * sine_part, values[..., 2 * quarter:]], axis=-1)


def reference(queries, new_keys, new_values, key_cache, value_cache, out_weight, lengths, page_table):
    offsets = jnp.arange(GROUP, dtype=jnp.int32)
    positions = lengths[:, None] + offsets[None, :]
    roped_keys = rotate(new_keys.astype(jnp.float32), positions).astype(jnp.bfloat16)
    roped_queries = rotate(queries.astype(jnp.float32).reshape(REQUESTS, GROUP, HEADS, HD), positions[:, :, None]).astype(jnp.bfloat16)
    fresh_slots = page_table[:, OLD_PAGES:].reshape(-1)
    key_cache_out = key_cache.at[fresh_slots].set(roped_keys.reshape(REQUESTS * NEW_PAGES, PAGE, HD))
    value_cache_out = value_cache.at[fresh_slots].set(new_values.reshape(REQUESTS * NEW_PAGES, PAGE, HD))
    window_index = jnp.arange(WINDOW, dtype=jnp.int32)
    score_scale = HD ** -0.5

    def one_request(inputs):
        query_block, fresh_keys, fresh_values, length, table_row = inputs
        old_keys = key_cache[table_row[:OLD_PAGES]].reshape(WINDOW, HD)
        old_values = value_cache[table_row[:OLD_PAGES]].reshape(WINDOW, HD)
        key_rows = jnp.concatenate([old_keys, fresh_keys], axis=0).astype(jnp.float32)
        value_rows = jnp.concatenate([old_values, fresh_values], axis=0).astype(jnp.float32)
        old_visible = (window_index[None, :] > offsets[:, None]) & ((length - WINDOW + window_index[None, :]) >= 0)
        new_visible = offsets[None, :] <= offsets[:, None]
        visible = jnp.concatenate([old_visible, new_visible], axis=1)
        scores = jnp.einsum("thd,kd->thk", query_block.astype(jnp.float32), key_rows) * score_scale
        scores = jnp.where(visible[:, None, :], scores, masked_score)
        row_max = jnp.max(scores, axis=2, keepdims=True)
        weights = jnp.where(visible[:, None, :], jnp.exp(scores - row_max), 0.0)
        row_total = jnp.sum(weights, axis=2, keepdims=True)
        rounded = lax.optimization_barrier(weights.astype(jnp.bfloat16))
        attended = jnp.einsum("thk,kd->thd", rounded.astype(jnp.float32), value_rows) / row_total
        attended = attended.astype(jnp.bfloat16).reshape(GROUP, HEADS * HD)
        return jnp.dot(attended, out_weight, preferred_element_type=jnp.float32).astype(jnp.bfloat16)

    hidden_states = lax.map(one_request, (roped_queries, roped_keys, new_values, lengths, page_table))
    return (hidden_states, key_cache_out, value_cache_out)
```

```python
import functools

import jax
import jax.numpy as jnp
from jax import lax
from jax.experimental import pallas as pl
from jax.experimental.pallas import tpu as pltpu
from jax.sharding import PartitionSpec as P

MESH = pl.DeviceIdType.MESH
NEG = -1e30
ANY = pl.BlockSpec(memory_space=pl.ANY)
VM = pl.BlockSpec(memory_space=pltpu.VMEM)
SM = pl.BlockSpec(memory_space=pltpu.SMEM)


def rope_tables(positions, quarter):
    freq_table = 10000.0 ** (-jnp.arange(quarter, dtype=jnp.float32) / quarter)
    angles = positions.astype(jnp.float32)[..., None] * freq_table
    cosine, sine = jnp.cos(angles), jnp.sin(angles)
    return (
        jnp.concatenate([cosine, cosine], axis=-1),
        jnp.concatenate([-sine, sine], axis=-1),
    )


def comm_kernel(
    dims,
    tab,
    fresh_k,
    fresh_v,
    kcache,
    vcache,
    kwin,
    vwin,
    newrecv,
    send_old,
    recv_old,
    comp_k,
    comp_v,
    qbuf_k,
    qbuf_v,
    send_new,
    s_old,
    r_old,
    s_fr,
    r_fr,
    s_q,
    r_q,
    s_ag,
    r_ag,
    s_new,
    r_new,
    loc,
):
    nb, ng, old_pages, mine = dims
    me = lax.axis_index("blk")
    g = lax.axis_index("group")

    barrier = pltpu.get_barrier_semaphore()

    def greet(k, _):
        pl.semaphore_signal(
            barrier, inc=1, device_id={"blk": lax.rem(me + k, nb), "group": g}, device_id_type=MESH
        )
        return 0

    lax.fori_loop(1, nb, greet, 0)
    for d in range(1, ng):
        pl.semaphore_signal(
            barrier, inc=1, device_id={"blk": me, "group": lax.rem(g + d, ng)}, device_id_type=MESH
        )

    def fill(a, _):
        i = tab[0, a]
        send_old[a, 0] = kcache[i]
        send_old[a, 1] = vcache[i]
        return 0

    lax.fori_loop(0, nb, fill, 0)
    recv_old[me] = send_old[me]
    pl.semaphore_wait(barrier, nb - 1 + ng - 1)

    def old_copy(k):
        a = lax.rem(me + k, nb)
        return pltpu.make_async_remote_copy(
            src_ref=send_old.at[a],
            dst_ref=recv_old.at[me],
            send_sem=s_old.at[a],
            recv_sem=r_old.at[me],
            device_id={"blk": a, "group": g},
            device_id_type=MESH,
        )

    def old_landed(k):
        a = lax.rem(me + nb - k, nb)
        return pltpu.make_async_remote_copy(
            src_ref=send_old.at[a],
            dst_ref=recv_old.at[a],
            send_sem=s_old.at[a],
            recv_sem=r_old.at[a],
            device_id={"blk": a, "group": g},
            device_id_type=MESH,
        )

    def start_old(k, _):
        old_copy(k).start()
        return 0

    lax.fori_loop(1, nb, start_old, 0)

    def quarter_copies(d):
        peer = lax.rem(g + d, ng)
        return [
            pltpu.make_async_remote_copy(
                src_ref=src.at[:, peer],
                dst_ref=dst.at[pl.ds(g * mine, mine)],
                send_sem=s_q.at[d, n],
                recv_sem=r_q.at[d, n],
                device_id={"blk": me, "group": peer},
                device_id_type=MESH,
            )
            for n, (src, dst) in enumerate(((fresh_k, qbuf_k), (fresh_v, qbuf_v)))
        ]

    def fresh_copies(d):
        peer = lax.rem(g + d, ng)
        return [
            pltpu.make_async_remote_copy(
                src_ref=src,
                dst_ref=dst.at[pl.ds(old_pages + g * mine, mine)],
                send_sem=s_fr.at[d, n],
                recv_sem=r_fr.at[d, n],
                device_id={"blk": me, "group": peer},
                device_id_type=MESH,
            )
            for n, (src, dst) in enumerate(((fresh_k, kwin), (fresh_v, vwin)))
        ]

    for d in range(1, ng):
        for c in quarter_copies(d):
            c.start()
    for d in range(1, ng):

        @pl.when(g + d < ng)
        def _():
            for c in fresh_copies(d):
                c.start()

    own = [
        pltpu.make_async_copy(src, dst.at[pl.ds(old_pages + g * mine, mine)], loc.at[n])
        for n, (src, dst) in enumerate(((fresh_k, kwin), (fresh_v, vwin)))
    ]
    for c in own:
        c.start()
    for i in range(mine):
        qbuf_k[g * mine + i] = fresh_k[i, g]
        qbuf_v[g * mine + i] = fresh_v[i, g]

    def wait_old(k, _):
        old_landed(k).wait_recv()
        return 0

    lax.fori_loop(1, nb, wait_old, 0)

    def pack(j, _):
        a = tab[1, j]
        comp_k[j] = recv_old[a, 0]
        comp_v[j] = recv_old[a, 1]
        return 0

    lax.fori_loop(0, old_pages, pack, 0)

    def window_copies(d, q):
        peer = lax.rem(g + d, ng)
        return [
            pltpu.make_async_remote_copy(
                src_ref=src.at[pl.ds(q * mine, mine)],
                dst_ref=dst.at[pl.ds(q * mine, mine), g],
                send_sem=s_ag.at[d, q, n],
                recv_sem=r_ag.at[d, q, n],
                device_id={"blk": me, "group": peer},
                device_id_type=MESH,
            )
            for n, (src, dst) in enumerate(((comp_k, kwin), (comp_v, vwin)))
        ]

    for q in range(ng):
        for d in range(1, ng):

            @pl.when(lax.rem(g + d, ng) <= q)
            def _():
                for c in window_copies(d, q):
                    c.start()

    own += [
        pltpu.make_async_copy(src, dst.at[pl.ds(0, old_pages), g], loc.at[2 + n])
        for n, (src, dst) in enumerate(((comp_k, kwin), (comp_v, vwin)))
    ]
    for c in own[2:]:
        c.start()

    def quarter_landed(d):
        peer = lax.rem(g + ng - d, ng)
        return [
            pltpu.make_async_remote_copy(
                src_ref=src.at[:, peer],
                dst_ref=dst.at[pl.ds(peer * mine, mine)],
                send_sem=s_q.at[d, n],
                recv_sem=r_q.at[d, n],
                device_id={"blk": me, "group": peer},
                device_id_type=MESH,
            )
            for n, (src, dst) in enumerate(((fresh_k, qbuf_k), (fresh_v, qbuf_v)))
        ]

    for d in range(1, ng):
        for c in quarter_landed(d):
            c.wait_recv()

    def fill_new(a, _):
        i = tab[2, a]
        send_new[a, 0] = qbuf_k[i]
        send_new[a, 1] = qbuf_v[i]
        return 0

    lax.fori_loop(0, nb, fill_new, 0)

    def new_copy(k):
        a = lax.rem(me + k, nb)
        return pltpu.make_async_remote_copy(
            src_ref=send_new.at[a],
            dst_ref=newrecv.at[me],
            send_sem=s_new.at[a],
            recv_sem=r_new.at[me],
            device_id={"blk": a, "group": g},
            device_id_type=MESH,
        )

    def new_landed(k):
        a = lax.rem(me + nb - k, nb)
        return pltpu.make_async_remote_copy(
            src_ref=send_new.at[a],
            dst_ref=newrecv.at[a],
            send_sem=s_new.at[a],
            recv_sem=r_new.at[a],
            device_id={"blk": a, "group": g},
            device_id_type=MESH,
        )

    def start_new(k, _):
        new_copy(k).start()
        return 0

    lax.fori_loop(1, nb, start_new, 0)
    own.append(pltpu.make_async_copy(send_new.at[me], newrecv.at[me], loc.at[4]))
    own[-1].start()

    def wait_sends(k, _):
        old_copy(k).wait_send()
        new_copy(k).wait_send()
        new_landed(k).wait_recv()
        return 0

    lax.fori_loop(1, nb, wait_sends, 0)
    for d in range(1, ng):
        for c in quarter_copies(d):
            c.wait_send()

        @pl.when(g + d < ng)
        def _():
            for c in fresh_copies(d):
                c.wait_send()

        @pl.when(g - d >= 0)
        def _():
            for c in fresh_copies(d):
                c.wait_recv()

    for q in range(ng):
        for d in range(1, ng):

            @pl.when(lax.rem(g + d, ng) <= q)
            def _():
                for c in window_copies(d, q):
                    c.wait_send()

            @pl.when(g <= q)
            def _():
                for c in window_copies(d, q):
                    c.wait_recv()

    for c in own:
        c.wait()


def attend_kernel(
    dims,
    tab,
    q_ref,
    cos_ref,
    sin_ref,
    kwin,
    vwin,
    w,
    kcache,
    vcache,
    newrecv,
    hidden,
    key_out,
    value_out,
    kbuf,
    vbuf,
    wbuf,
    qs,
    att,
    kpages,
    vpages,
    sem,
    page_sem,
    out_sem,
):
    nb, ng, tok, heads, hd, tile, scale, wchunk = dims
    g = lax.axis_index("group")
    win = kbuf.shape[0]
    keys = win - tok + tile
    half = hd // 2
    quarter = half // 2

    kv = [
        pltpu.make_async_copy(src.at[pl.ds(g * tok, win)], dst, sem.at[n])
        for n, (src, dst) in enumerate(((kwin, kbuf), (vwin, vbuf)))
    ]
    for c in kv:
        c.start()
    pool = [
        pltpu.make_async_copy(kcache, kpages, sem.at[2]),
        pltpu.make_async_copy(vcache, vpages, sem.at[3]),
    ]
    for c in pool:
        c.start()
    weight = pltpu.make_async_copy(w, wbuf, sem.at[4])
    weight.start()

    for t in range(tok // tile):
        rows = pl.ds(t * tile, tile)
        cosine, sine = cos_ref[rows, :], sin_ref[rows, :]
        for h in range(heads):
            lead = q_ref[rows, h * hd : h * hd + half].astype(jnp.float32)
            turned = pltpu.roll(lead, quarter, axis=1)
            roped = (lead * cosine + turned * sine).astype(jnp.bfloat16)
            qs[t, h * tile : (h + 1) * tile, :half] = roped * scale
            qs[t, h * tile : (h + 1) * tile, half:] = (
                q_ref[rows, h * hd + half : (h + 1) * hd] * scale
            )

    for c in pool:
        c.wait()

    def place(b, _):
        i = tab[3, b]

        @pl.when(i >= 0)
        def _():
            a = pltpu.make_async_copy(newrecv.at[b, 0], kpages.at[i], page_sem.at[b, 0])
            c = pltpu.make_async_copy(newrecv.at[b, 1], vpages.at[i], page_sem.at[b, 1])
            a.start()
            c.start()

        return 0

    lax.fori_loop(0, nb, place, 0)

    def placed(b, _):
        i = tab[3, b]

        @pl.when(i >= 0)
        def _():
            pltpu.make_async_copy(newrecv.at[b, 0], kpages.at[i], page_sem.at[b, 0]).wait()
            pltpu.make_async_copy(newrecv.at[b, 1], vpages.at[i], page_sem.at[b, 1]).wait()

        return 0

    for c in kv:
        c.wait()

    pair = 2 * tile
    first_fresh = win - tok - g * tok

    def run(with_old):
        def step(it, _):
            t = it // (heads // 2)
            hp = it % (heads // 2)
            q = qs[t, pl.ds(hp * pair, pair), :]
            start = pl.multiple_of(t * tile, tile)
            k = kbuf[pl.ds(start, keys), :]
            s = lax.dot_general(q, k, (((1,), (1,)), ((), ())), preferred_element_type=jnp.float32)
            r = lax.rem(lax.broadcasted_iota(jnp.int32, (pair, tile), 0), tile)
            c = lax.broadcasted_iota(jnp.int32, (pair, tile), 1)
            s = jnp.concatenate(
                [
                    jnp.where(c > r, s[:, :tile], NEG),
                    s[:, tile : keys - tile],
                    jnp.where(c <= r, s[:, keys - tile :], NEG),
                ],
                axis=1,
            )
            if not with_old:
                col = start + lax.broadcasted_iota(jnp.int32, (1, keys), 1)
                s = jnp.where(col >= first_fresh, s, NEG)
            m = jnp.max(s, axis=1, keepdims=True)
            p = jnp.exp(s - m)
            total = jnp.sum(p, axis=1, keepdims=True)
            o = jnp.dot(
                p.astype(jnp.bfloat16),
                vbuf[pl.ds(start, keys), :],
                preferred_element_type=jnp.float32,
            )
            o = (o / total).astype(jnp.bfloat16)
            rows = pl.ds(start, tile)
            col0 = pl.multiple_of(hp * 2 * hd, hd)
            att[rows, pl.ds(col0, hd)] = o[:tile]
            att[rows, pl.ds(pl.multiple_of(col0 + hd, hd), hd)] = o[tile:]
            return 0

        lax.fori_loop(0, (tok // tile) * (heads // 2), step, 0)

    length = tab[4, 0]

    @pl.when(length > 0)
    def _():
        run(True)

    @pl.when(length <= 0)
    def _():
        run(False)

    lax.fori_loop(0, nb, placed, 0)
    outs = [
        pltpu.make_async_copy(kpages, key_out, out_sem.at[0]),
        pltpu.make_async_copy(vpages, value_out, out_sem.at[1]),
    ]
    for c in outs:
        c.start()
    weight.wait()

    def project(n, _):
        cols = pl.ds(pl.multiple_of(n * wchunk, wchunk), wchunk)
        hidden[:, cols] = jnp.dot(
            att[...], wbuf[:, cols], preferred_element_type=jnp.float32
        ).astype(jnp.bfloat16)
        return 0

    lax.fori_loop(0, w.shape[1] // wchunk, project, 0)
    for c in outs:
        c.wait()


def body(queries, new_keys, new_values, key_cache, value_cache, out_weight, lengths, page_table):
    nb = lax.axis_size("blk")
    ng = lax.axis_size("group")
    me = lax.axis_index("blk")
    g = lax.axis_index("group")
    tok = queries.shape[1]
    hd = new_keys.shape[2]
    heads = queries.shape[2] // hd
    pages_here, rows = key_cache.shape[:2]
    slots = page_table.shape[1]
    group_len = tok * ng
    fresh = group_len // (rows * ng)
    old = slots - fresh
    mine = fresh // ng
    bf16 = jnp.bfloat16

    length = lengths[me]
    positions = length + g * tok + jnp.arange(tok, dtype=jnp.int32)
    cosine, sine = rope_tables(positions, hd // 4)
    half = hd // 2
    lead = new_keys[0, :, :half].astype(jnp.float32)
    turned = jnp.concatenate([lead[:, half // 2 :], lead[:, : half // 2]], axis=1)
    roped = jnp.concatenate(
        [(lead * cosine + turned * sine).astype(bf16), new_keys[0, :, half:]], axis=1
    )

    owner = page_table // pages_here
    local = page_table % pages_here
    here = owner == me
    my_owner = owner[me]
    ids = jnp.arange(nb, dtype=jnp.int32)
    wanted = jnp.sum(jnp.where(here[:, :old], local[:, :old], 0), axis=1)
    target = jnp.sum(jnp.where(here[:, old:], local[:, old:] + 1, 0), axis=1) - 1
    source = jnp.sum(
        jnp.where(
            my_owner[None, old:] == ids[:, None], jnp.arange(fresh, dtype=jnp.int32)[None, :], 0
        ),
        axis=1,
    )
    tab = jnp.stack(
        [wanted, jnp.pad(my_owner[:old], (0, nb - old)), source, target, jnp.full((nb,), length)]
    ).astype(jnp.int32)

    shape4 = (mine, ng, rows, hd)
    kwin, vwin, newrecv = pl.pallas_call(
        functools.partial(comm_kernel, (nb, ng, old, mine)),
        out_shape=(
            jax.ShapeDtypeStruct((old + fresh, ng, rows, hd), bf16),
            jax.ShapeDtypeStruct((old + fresh, ng, rows, hd), bf16),
            jax.ShapeDtypeStruct((nb, 2, rows, hd), bf16),
        ),
        in_specs=[SM, VM, VM, VM, VM],
        out_specs=(ANY, ANY, ANY),
        scratch_shapes=[
            pltpu.VMEM((nb, 2, rows, hd), bf16),
            pltpu.VMEM((nb, 2, rows, hd), bf16),
            pltpu.VMEM((old, rows, hd), bf16),
            pltpu.VMEM((old, rows, hd), bf16),
            pltpu.VMEM((fresh, rows, hd), bf16),
            pltpu.VMEM((fresh, rows, hd), bf16),
            pltpu.VMEM((nb, 2, rows, hd), bf16),
            pltpu.SemaphoreType.DMA((nb,)),
            pltpu.SemaphoreType.DMA((nb,)),
            pltpu.SemaphoreType.DMA((ng, 2)),
            pltpu.SemaphoreType.DMA((ng, 2)),
            pltpu.SemaphoreType.DMA((ng, 2)),
            pltpu.SemaphoreType.DMA((ng, 2)),
            pltpu.SemaphoreType.DMA((ng, ng, 2)),
            pltpu.SemaphoreType.DMA((ng, ng, 2)),
            pltpu.SemaphoreType.DMA((nb,)),
            pltpu.SemaphoreType.DMA((nb,)),
            pltpu.SemaphoreType.DMA((5,)),
        ],
        compiler_params=pltpu.CompilerParams(collective_id=0, has_side_effects=True),
        name="exchange",
    )(tab, roped.reshape(shape4), new_values[0].reshape(shape4), key_cache, value_cache)

    tile = rows * ng
    win = old * tile + tok
    d_out = out_weight.shape[1]
    hidden, key_out, value_out = pl.pallas_call(
        functools.partial(attend_kernel, (nb, ng, tok, heads, hd, tile, hd**-0.5, 512)),
        out_shape=(
            jax.ShapeDtypeStruct((tok, d_out), bf16),
            jax.ShapeDtypeStruct(key_cache.shape, bf16),
            jax.ShapeDtypeStruct(value_cache.shape, bf16),
        ),
        in_specs=[SM, VM, VM, VM, ANY, ANY, ANY, ANY, ANY, ANY],
        out_specs=(VM, ANY, ANY),
        scratch_shapes=[
            pltpu.VMEM((win, hd), bf16),
            pltpu.VMEM((win, hd), bf16),
            pltpu.VMEM(out_weight.shape, bf16),
            pltpu.VMEM((tok // tile, heads * tile, hd), bf16),
            pltpu.VMEM((tok, heads * hd), bf16),
            pltpu.VMEM(key_cache.shape, bf16),
            pltpu.VMEM(value_cache.shape, bf16),
            pltpu.SemaphoreType.DMA((5,)),
            pltpu.SemaphoreType.DMA((nb, 2)),
            pltpu.SemaphoreType.DMA((2,)),
        ],
        compiler_params=pltpu.CompilerParams(vmem_limit_bytes=60 << 20),
        name="attend",
    )(
        tab,
        queries[0],
        cosine,
        sine,
        kwin.reshape(-1, hd),
        vwin.reshape(-1, hd),
        out_weight,
        key_cache,
        value_cache,
        newrecv,
    )
    return (hidden[None], key_out, value_out)


def solution(mesh):
    split = P("blk", "group", None)
    return jax.shard_map(
        body,
        mesh=mesh,
        in_specs=(split, split, split, split, split, P(), P(), P()),
        out_specs=(split, split, split),
        check_vma=False,
    )
```

```python
import functools

import jax
import jax.numpy as jnp
from jax import lax
from jax.experimental import pallas as pl
from jax.experimental.pallas import tpu as pltpu
from jax.sharding import PartitionSpec as P

MESH = pl.DeviceIdType.MESH
NEG = -1e30
ANY = pl.BlockSpec(memory_space=pl.ANY)
VM = pl.BlockSpec(memory_space=pltpu.VMEM)
SM = pl.BlockSpec(memory_space=pltpu.SMEM)


def rope_tables(positions, quarter):
    freq_table = 10000.0 ** (-jnp.arange(quarter, dtype=jnp.float32) / quarter)
    angles = positions.astype(jnp.float32)[..., None] * freq_table
    cosine, sine = jnp.cos(angles), jnp.sin(angles)
    return (
        jnp.concatenate([cosine, cosine], axis=-1),
        jnp.concatenate([-sine, sine], axis=-1),
    )


def layer_kernel(
    dims,
    tab,
    queries,
    fresh_k,
    fresh_v,
    kcache,
    vcache,
    cos_ref,
    sin_ref,
    attended,
    newrecv,
    q_ref,
    qs,
    att,
    kbuf,
    vbuf,
    send_old,
    recv_k,
    recv_v,
    comp,
    qbuf,
    send_new,
    score0,
    score1,
    s_old,
    r_old,
    s_fr,
    r_fr,
    s_q,
    r_q,
    s_ag,
    r_ag,
    s_new,
    r_new,
    loc,
    out_sem,
):
    nb, ng, old_pages, mine, heads, hd, scale = dims
    me = lax.axis_index("blk")
    g = lax.axis_index("group")
    core = lax.rem(g, 2)
    hi = g // 2
    partner = 2 * hi + 1 - core
    across = 2 * (1 - hi) + core
    other = 2 * (1 - hi)
    windows = (kbuf, vbuf)
    fresh = (fresh_k, fresh_v)
    caches = (kcache, vcache)
    recv_old = (recv_k, recv_v)
    rows = kcache.shape[1]
    tile = rows * ng
    half = hd // 2
    quarter = half // 2

    def remote(src, dst, ssem, rsem, blk, grp):
        return pltpu.make_async_remote_copy(
            src_ref=src,
            dst_ref=dst,
            send_sem=ssem,
            recv_sem=rsem,
            device_id={"blk": blk, "group": grp},
            device_id_type=MESH,
        )

    get_q = pltpu.make_async_copy(queries, q_ref, loc.at[0])
    get_q.start()

    barrier = pltpu.get_barrier_semaphore()

    def greet(k, _):
        pl.semaphore_signal(
            barrier, inc=1, device_id={"blk": lax.rem(me + k, nb), "group": g}, device_id_type=MESH
        )
        return 0

    lax.fori_loop(1, nb, greet, 0)
    for d in range(1, ng):
        pl.semaphore_signal(
            barrier, inc=1, device_id={"blk": me, "group": lax.rem(g + d, ng)}, device_id_type=MESH
        )

    for n in range(2):

        def fill(a, _):
            send_old[n, a] = caches[n][tab[0, a]]
            return 0

        lax.fori_loop(0, nb, fill, 0)
        recv_old[n][me] = send_old[n, me]
    pl.semaphore_wait(barrier, nb - 1 + ng - 1)

    def old_copy(n, k):
        a = lax.rem(me + k, nb)
        return remote(
            send_old.at[n, a], recv_old[n].at[me], s_old.at[n, a], r_old.at[n, me], a, g
        )

    def old_landed(n, k):
        a = lax.rem(me + nb - k, nb)
        return remote(send_old.at[n, a], recv_old[n].at[a], s_old.at[n, a], r_old.at[n, a], a, g)

    for n in range(2):

        def start_old(k, _):
            old_copy(n, k).start()
            return 0

        lax.fori_loop(1, nb, start_old, 0)

    def fresh_at(src, dst):
        return pl.ds(old_pages + mine * (src - dst), mine)

    def fresh_near(n):
        return remote(
            fresh[n], windows[n].at[fresh_at(g, partner)], s_fr.at[n, 0], r_fr.at[n, g], me, partner
        )

    def fresh_far(n):
        return remote(
            fresh[n], windows[n].at[fresh_at(g, across)], s_fr.at[n, 1], r_fr.at[n, g], me, across
        )

    def fresh_pass(n):
        return remote(
            windows[n].at[fresh_at(across, g)],
            windows[n].at[fresh_at(across, partner)],
            s_fr.at[n, 2],
            r_fr.at[n, across],
            me,
            partner,
        )

    def fresh_from(n, src):
        return remote(
            fresh[n], windows[n].at[fresh_at(src, g)], s_fr.at[n, 0], r_fr.at[n, src], me, partner
        )

    def quarter_to(n, dst):
        return remote(
            fresh[n].at[:, dst],
            qbuf.at[n, pl.ds(mine * g, mine)],
            s_q.at[n, dst],
            r_q.at[n, g],
            me,
            dst,
        )

    def quarter_from(n, src):
        return remote(
            fresh[n].at[:, g],
            qbuf.at[n, pl.ds(mine * src, mine)],
            s_q.at[n, g],
            r_q.at[n, src],
            me,
            partner,
        )

    @pl.when(hi == 0)
    def _():
        for n in range(2):
            fresh_far(n).start()

    @pl.when(core == 0)
    def _():
        for n in range(2):
            fresh_near(n).start()

    for d in range(ng - 1):

        @pl.when(g > d)
        def _():
            for n in range(2):
                quarter_to(n, d).start()

    for n in range(2):
        windows[n][pl.ds(old_pages, mine)] = fresh[n][...]
        qbuf[n, pl.ds(mine * g, mine)] = fresh[n][:, g]

    get_q.wait()
    tiles = q_ref.shape[0] // tile
    for t in range(tiles):
        trows = pl.ds(t * tile, tile)
        cosine, sine = cos_ref[trows, :], sin_ref[trows, :]
        for h in range(heads):
            lead = q_ref[trows, h * hd : h * hd + half].astype(jnp.float32)
            turned = pltpu.roll(lead, quarter, axis=1)
            roped = (lead * cosine + turned * sine).astype(jnp.bfloat16)
            qs[t, h * tile : (h + 1) * tile, :half] = roped * scale
            qs[t, h * tile : (h + 1) * tile, half:] = (
                q_ref[trows, h * hd + half : (h + 1) * hd] * scale
            )

    def block(q, dst):
        return pl.ds(mine * (q - dst), mine)

    def ag_near(n, q):
        return remote(
            comp.at[n, pl.ds(mine * q, mine)],
            windows[n].at[block(q, partner), g],
            s_ag.at[n, q, 0],
            r_ag.at[n, q, g],
            me,
            partner,
        )

    def ag_far(n, q, dst):
        return remote(
            comp.at[n, pl.ds(mine * q, mine)],
            windows[n].at[block(q, dst), g],
            s_ag.at[n, q, 1],
            r_ag.at[n, q, g],
            me,
            dst,
        )

    def ag_pass(n, q):
        return remote(
            windows[n].at[block(q, g), across],
            windows[n].at[block(q, partner), across],
            s_ag.at[n, q, 2],
            r_ag.at[n, q, across],
            me,
            partner,
        )

    def ag_from(n, q, src):
        return remote(
            comp.at[n, pl.ds(mine * q, mine)],
            windows[n].at[block(q, g), src],
            s_ag.at[n, q, 0],
            r_ag.at[n, q, src],
            me,
            partner,
        )

    def far_do(n, q, act):
        @pl.when(other + 1 <= q)
        def _():
            act(ag_far(n, q, across))

        @pl.when(other == q)
        def _():
            act(ag_far(n, q, other))

    def start(c):
        c.start()

    def sent(c):
        c.wait_send()

    for n in range(2):

        def wait_old(k, _):
            old_landed(n, k).wait_recv()
            return 0

        lax.fori_loop(1, nb, wait_old, 0)

        def pack(j, _):
            comp[n, j] = recv_old[n][tab[1, j]]
            return 0

        lax.fori_loop(0, old_pages, pack, 0)
        for q in range(ng):
            far_do(n, q, start)

            @pl.when(partner <= q)
            def _():
                ag_near(n, q).start()

            @pl.when(g <= q)
            def _():
                windows[n][block(q, g), g] = comp[n, pl.ds(mine * q, mine)]

        if n == 0:

            @pl.when(hi == 1)
            def _():
                for m in range(2):
                    fresh_from(m, across).wait_recv()
                    fresh_pass(m).start()

    @pl.when(core == 1)
    def _():
        for n in range(2):
            fresh_from(n, partner).wait_recv()

    @pl.when(hi == 1)
    def _():
        for n in range(2):
            fresh_from(n, 1 - core).wait_recv()

    for src in range(ng):

        @pl.when(src < g)
        def _():
            for n in range(2):
                qbuf[n, pl.ds(mine * src, mine)] = windows[n][fresh_at(src, g), g]

        @pl.when(src > g)
        def _():
            for n in range(2):
                quarter_from(n, src).wait_recv()

    def fill_new(a, _):
        i = tab[2, a]
        send_new[a, 0] = qbuf[0, i]
        send_new[a, 1] = qbuf[1, i]
        return 0

    lax.fori_loop(0, nb, fill_new, 0)

    def new_copy(k):
        a = lax.rem(me + k, nb)
        return remote(send_new.at[a], newrecv.at[me], s_new.at[a], r_new.at[me], a, g)

    def new_landed(k):
        a = lax.rem(me + nb - k, nb)
        return remote(send_new.at[a], newrecv.at[a], s_new.at[a], r_new.at[a], a, g)

    def start_new(k, _):
        new_copy(k).start()
        return 0

    lax.fori_loop(1, nb, start_new, 0)
    keep = pltpu.make_async_copy(send_new.at[me], newrecv.at[me], loc.at[1])
    keep.start()

    for n in range(2):
        for q in range(ng):

            @pl.when(2 * hi + 1 <= q)
            def _():
                ag_from(n, q, across).wait_recv()
                ag_pass(n, q).start()

    for n in range(2):
        for q in range(ng):

            @pl.when(g <= q)
            def _():
                ag_from(n, q, partner).wait_recv()
                ag_from(n, q, other + 1 - core).wait_recv()

            @pl.when(2 * hi == q)
            def _():
                @pl.when(core == 0)
                def _():
                    ag_from(n, q, across).wait_recv()

    parts = 2
    group = heads // parts
    high = group * tile
    total_parts = tiles * parts
    pages = old_pages + 1
    keys = pages * tile
    empty = tab[4, 0] <= 0

    def scores(it, dst):
        t = it // parts
        first = pl.multiple_of(lax.rem(it, parts) * high, high)
        k = kbuf[pl.ds(t, pages)].reshape(keys, hd)
        dst[...] = lax.dot_general(
            qs[t, pl.ds(first, high), :],
            k,
            (((1,), (1,)), ((), ())),
            preferred_element_type=jnp.float32,
        )

    def softmax(it, src):
        t = it // parts
        part = lax.rem(it, parts)
        r = lax.rem(lax.broadcasted_iota(jnp.int32, (high, tile), 0), tile)
        c = lax.broadcasted_iota(jnp.int32, (high, tile), 1)
        s = jnp.concatenate(
            [
                jnp.where(c > r, src[:, :tile], NEG),
                src[:, tile : keys - tile],
                jnp.where(c <= r, src[:, keys - tile :], NEG),
            ],
            axis=1,
        )
        col = (t + mine * g) * tile + lax.broadcasted_iota(jnp.int32, (1, keys), 1)
        hidden_key = jnp.logical_and(col < old_pages * tile, empty)
        s = jnp.where(hidden_key, NEG, s)
        m = jnp.max(s, axis=1, keepdims=True)
        p = jnp.exp(s - m)
        total = jnp.sum(p, axis=1, keepdims=True)
        o = jnp.dot(
            p.astype(jnp.bfloat16),
            vbuf[pl.ds(t, pages)].reshape(keys, hd),
            preferred_element_type=jnp.float32,
        )
        o = (o / total).astype(jnp.bfloat16)
        at = pl.ds(pl.multiple_of(t * tile, tile), tile)
        for h in range(group):
            cols = pl.ds(pl.multiple_of((part * group + h) * hd, hd), hd)
            att[at, cols] = o[h * tile : (h + 1) * tile]

    scores(0, score0)

    def step(i, _):
        scores(2 * i + 1, score1)
        softmax(2 * i, score0)
        scores(lax.rem(2 * i + 2, total_parts), score0)
        softmax(2 * i + 1, score1)
        return 0

    lax.fori_loop(0, total_parts // 2, step, 0)
    put = pltpu.make_async_copy(att, attended, out_sem.at[0])
    put.start()

    def wait_rest(k, _):
        old_copy(0, k).wait_send()
        old_copy(1, k).wait_send()
        new_copy(k).wait_send()
        new_landed(k).wait_recv()
        return 0

    lax.fori_loop(1, nb, wait_rest, 0)
    keep.wait()

    @pl.when(hi == 0)
    def _():
        for n in range(2):
            fresh_far(n).wait_send()

    @pl.when(core == 0)
    def _():
        for n in range(2):
            fresh_near(n).wait_send()

    @pl.when(hi == 1)
    def _():
        for n in range(2):
            fresh_pass(n).wait_send()

    for n in range(2):
        for d in range(ng - 1):

            @pl.when(g > d)
            def _():
                quarter_to(n, d).wait_send()

        for q in range(ng):
            far_do(n, q, sent)

            @pl.when(partner <= q)
            def _():
                ag_near(n, q).wait_send()

            @pl.when(2 * hi + 1 <= q)
            def _():
                ag_pass(n, q).wait_send()

    put.wait()


def project_kernel(
    nb, tab, att, w, kcache, vcache, newrecv, hidden, key_out, value_out, pages, sem, page_sem
):
    n = pl.program_id(0)
    caches = (kcache, vcache)
    outs = (key_out, value_out)

    @pl.when(n == 0)
    def _():
        for i in range(2):
            pltpu.make_async_copy(caches[i], pages.at[i], sem.at[i]).start()

    def place(b, act):
        i = tab[3, b]

        @pl.when(i >= 0)
        def _():
            for m in range(2):
                act(
                    pltpu.make_async_copy(newrecv.at[b, m], pages.at[m, i], page_sem.at[b, m])
                )

    @pl.when(n == 1)
    def _():
        for i in range(2):
            pltpu.make_async_copy(caches[i], pages.at[i], sem.at[i]).wait()

        def go(b, _):
            place(b, lambda c: c.start())
            return 0

        lax.fori_loop(0, nb, go, 0)

    @pl.when(n == 2)
    def _():
        def done(b, _):
            place(b, lambda c: c.wait())
            return 0

        lax.fori_loop(0, nb, done, 0)
        for i in range(2):
            pltpu.make_async_copy(pages.at[i], outs[i], sem.at[2 + i]).start()

    hidden[...] = jnp.dot(att[...], w[...], preferred_element_type=jnp.float32).astype(
        jnp.bfloat16
    )

    @pl.when(n == pl.num_programs(0) - 1)
    def _():
        for i in range(2):
            pltpu.make_async_copy(pages.at[i], outs[i], sem.at[2 + i]).wait()


def body(queries, new_keys, new_values, key_cache, value_cache, out_weight, lengths, page_table):
    nb = lax.axis_size("blk")
    ng = lax.axis_size("group")
    me = lax.axis_index("blk")
    g = lax.axis_index("group")
    tok = queries.shape[1]
    hd = new_keys.shape[2]
    heads = queries.shape[2] // hd
    pages_here, rows = key_cache.shape[:2]
    slots = page_table.shape[1]
    group_len = tok * ng
    fresh = group_len // (rows * ng)
    old = slots - fresh
    mine = fresh // ng
    bf16 = jnp.bfloat16

    length = lengths[me]
    positions = length + g * tok + jnp.arange(tok, dtype=jnp.int32)
    cosine, sine = rope_tables(positions, hd // 4)
    half = hd // 2
    lead = new_keys[0, :, :half].astype(jnp.float32)
    turned = jnp.concatenate([lead[:, half // 2 :], lead[:, : half // 2]], axis=1)
    roped = jnp.concatenate(
        [(lead * cosine + turned * sine).astype(bf16), new_keys[0, :, half:]], axis=1
    )

    owner = page_table // pages_here
    local = page_table % pages_here
    here = owner == me
    my_owner = owner[me]
    ids = jnp.arange(nb, dtype=jnp.int32)
    wanted = jnp.sum(jnp.where(here[:, :old], local[:, :old], 0), axis=1)
    target = jnp.sum(jnp.where(here[:, old:], local[:, old:] + 1, 0), axis=1) - 1
    source = jnp.sum(
        jnp.where(
            my_owner[None, old:] == ids[:, None], jnp.arange(fresh, dtype=jnp.int32)[None, :], 0
        ),
        axis=1,
    )
    tab = jnp.stack(
        [wanted, jnp.pad(my_owner[:old], (0, nb - old)), source, target, jnp.full((nb,), length)]
    ).astype(jnp.int32)

    shape4 = (mine, ng, rows, hd)
    tile = rows * ng
    keys = (old + 1) * tile
    dma = pltpu.SemaphoreType.DMA
    attended, newrecv = pl.pallas_call(
        functools.partial(layer_kernel, (nb, ng, old, mine, heads, hd, hd**-0.5)),
        out_shape=(
            jax.ShapeDtypeStruct((tok, heads * hd), bf16),
            jax.ShapeDtypeStruct((nb, 2, rows, hd), bf16),
        ),
        in_specs=[SM, ANY, VM, VM, VM, VM, VM, VM],
        out_specs=(ANY, ANY),
        scratch_shapes=[
            pltpu.VMEM((tok, heads * hd), bf16),
            pltpu.VMEM((tok // tile, heads * tile, hd), bf16),
            pltpu.VMEM((tok, heads * hd), bf16),
            pltpu.VMEM((old + mine, ng, rows, hd), bf16),
            pltpu.VMEM((old + mine, ng, rows, hd), bf16),
            pltpu.VMEM((2, nb, rows, hd), bf16),
            pltpu.VMEM((nb, rows, hd), bf16),
            pltpu.VMEM((nb, rows, hd), bf16),
            pltpu.VMEM((2, old, rows, hd), bf16),
            pltpu.VMEM((2, fresh, rows, hd), bf16),
            pltpu.VMEM((nb, 2, rows, hd), bf16),
            pltpu.VMEM((heads // 2 * tile, keys), jnp.float32),
            pltpu.VMEM((heads // 2 * tile, keys), jnp.float32),
            dma((2, nb)),
            dma((2, nb)),
            dma((2, 3)),
            dma((2, ng)),
            dma((2, ng)),
            dma((2, ng)),
            dma((2, ng, 3)),
            dma((2, ng, ng)),
            dma((nb,)),
            dma((nb,)),
            dma((2,)),
            dma((1,)),
        ],
        compiler_params=pltpu.CompilerParams(
            collective_id=0, has_side_effects=True, vmem_limit_bytes=60 << 20
        ),
        name="layer",
    )(
        tab,
        queries[0],
        roped.reshape(shape4),
        new_values[0].reshape(shape4),
        key_cache,
        value_cache,
        cosine,
        sine,
    )

    d_out = out_weight.shape[1]
    chunk = d_out // 5
    hidden, key_out, value_out = pl.pallas_call(
        functools.partial(project_kernel, nb),
        grid=(d_out // chunk,),
        out_shape=(
            jax.ShapeDtypeStruct((tok, d_out), bf16),
            jax.ShapeDtypeStruct(key_cache.shape, bf16),
            jax.ShapeDtypeStruct(value_cache.shape, bf16),
        ),
        in_specs=[
            SM,
            pl.BlockSpec((tok, heads * hd), lambda n: (0, 0)),
            pl.BlockSpec((heads * hd, chunk), lambda n: (0, n)),
            ANY,
            ANY,
            ANY,
        ],
        out_specs=(pl.BlockSpec((tok, chunk), lambda n: (0, n)), ANY, ANY),
        scratch_shapes=[
            pltpu.VMEM((2, *key_cache.shape), bf16),
            dma((4,)),
            dma((nb, 2)),
        ],
        compiler_params=pltpu.CompilerParams(vmem_limit_bytes=60 << 20),
        name="project",
    )(tab, attended, out_weight, key_cache, value_cache, newrecv)
    return (hidden[None], key_out, value_out)


def solution(mesh):
    split = P("blk", "group", None)
    return jax.shard_map(
        body,
        mesh=mesh,
        in_specs=(split, split, split, split, split, P(), P(), P()),
        out_specs=(split, split, split),
        check_vma=False,
    )
```

```python
import functools

import jax
import jax.numpy as jnp
from jax import lax
from jax.experimental import pallas as pl
from jax.experimental.pallas import tpu as pltpu
from jax.sharding import PartitionSpec as P

MESH = pl.DeviceIdType.MESH
NEG = -1e30
ANY = pl.BlockSpec(memory_space=pl.ANY)
VM = pl.BlockSpec(memory_space=pltpu.VMEM)
SM = pl.BlockSpec(memory_space=pltpu.SMEM)


def layer_kernel(
    dims,
    tab,
    table,
    lengths,
    freq,
    new_k,
    fresh_v,
    kcache,
    vcache,
    queries,
    weight,
    hidden,
    key_out,
    value_out,
    fresh_k,
    cos_ref,
    sin_ref,
    q_ref,
    wbuf,
    qs,
    hid,
    pages,
    newrecv,
    kbuf,
    vbuf,
    send_old,
    recv_k,
    recv_v,
    comp,
    qbuf,
    send_new,
    score0,
    score1,
    prob0,
    prob1,
    sums0,
    sums1,
    s_old,
    r_old,
    s_fr,
    r_fr,
    s_q,
    r_q,
    s_ag,
    r_ag,
    s_new,
    r_new,
    loc,
    out_sem,
    w_sem,
):
    nb, ng, old_pages, mine, heads, hd, scale = dims
    pages_here = kcache.shape[0]
    me = lax.axis_index("blk")
    g = lax.axis_index("group")
    core = lax.rem(g, 2)
    hi = g // 2
    partner = 2 * hi + 1 - core
    across = 2 * (1 - hi) + core
    other = 2 * (1 - hi)
    windows = (kbuf, vbuf)
    fresh = (fresh_k, fresh_v)
    caches = (kcache, vcache)
    recv_old = (recv_k, recv_v)
    rows = kcache.shape[1]
    tile = rows * ng
    half = hd // 2
    quarter = half // 2

    def remote(src, dst, ssem, rsem, blk, grp):
        return pltpu.make_async_remote_copy(
            src_ref=src,
            dst_ref=dst,
            send_sem=ssem,
            recv_sem=rsem,
            device_id={"blk": blk, "group": grp},
            device_id_type=MESH,
        )

    get_q = pltpu.make_async_copy(queries, q_ref, loc.at[0])
    get_q.start()
    chunks = 5
    slots = wbuf.shape[0]
    wide = wbuf.shape[2]

    def get_w(n):
        cols = pl.ds(pl.multiple_of(n * wide, wide), wide)
        return pltpu.make_async_copy(
            weight.at[:, cols], wbuf.at[lax.rem(n, slots)], w_sem.at[lax.rem(n, slots)]
        )

    for n in range(slots):
        get_w(jnp.int32(n)).start()

    barrier = pltpu.get_barrier_semaphore()

    def greet(k, _):
        pl.semaphore_signal(
            barrier, inc=1, device_id={"blk": lax.rem(me + k, nb), "group": g}, device_id_type=MESH
        )
        return 0

    lax.fori_loop(1, nb, greet, 0)
    for d in range(1, ng):
        pl.semaphore_signal(
            barrier, inc=1, device_id={"blk": me, "group": lax.rem(g + d, ng)}, device_id_type=MESH
        )

    for n in range(2):

        def fill(a, _):
            send_old[n, a] = caches[n][tab[a]]
            return 0

        lax.fori_loop(0, nb, fill, 0)
        recv_old[n][me] = send_old[n, me]
    pl.semaphore_wait(barrier, nb - 1 + ng - 1)

    def old_copy(n, k):
        a = lax.rem(me + k, nb)
        return remote(
            send_old.at[n, a], recv_old[n].at[me], s_old.at[n, a], r_old.at[n, me], a, g
        )

    def old_landed(n, k):
        a = lax.rem(me + nb - k, nb)
        return remote(send_old.at[n, a], recv_old[n].at[a], s_old.at[n, a], r_old.at[n, a], a, g)

    for n in range(2):

        def start_old(k, _):
            old_copy(n, k).start()
            return 0

        lax.fori_loop(1, nb, start_old, 0)

    def fresh_at(src, dst):
        return pl.ds(old_pages + mine * (src - dst), mine)

    def fresh_near(n):
        return remote(
            fresh[n], windows[n].at[fresh_at(g, partner)], s_fr.at[n, 0], r_fr.at[n, g], me, partner
        )

    def fresh_far(n):
        return remote(
            fresh[n], windows[n].at[fresh_at(g, across)], s_fr.at[n, 1], r_fr.at[n, g], me, across
        )

    def fresh_pass(n):
        return remote(
            windows[n].at[fresh_at(across, g)],
            windows[n].at[fresh_at(across, partner)],
            s_fr.at[n, 2],
            r_fr.at[n, across],
            me,
            partner,
        )

    def fresh_from(n, src):
        return remote(
            fresh[n], windows[n].at[fresh_at(src, g)], s_fr.at[n, 0], r_fr.at[n, src], me, partner
        )

    def quarter_to(n, dst):
        return remote(
            fresh[n].at[:, dst],
            qbuf.at[n, pl.ds(mine * g, mine)],
            s_q.at[n, dst],
            r_q.at[n, g],
            me,
            dst,
        )

    def quarter_from(n, src):
        return remote(
            fresh[n].at[:, g],
            qbuf.at[n, pl.ds(mine * src, mine)],
            s_q.at[n, g],
            r_q.at[n, src],
            me,
            partner,
        )

    def send_fresh(n):
        @pl.when(hi == 0)
        def _():
            fresh_far(n).start()

        @pl.when(core == 0)
        def _():
            fresh_near(n).start()

        for d in range(ng - 1):

            @pl.when(g > d)
            def _():
                quarter_to(n, d).start()

        windows[n][pl.ds(old_pages, mine)] = fresh[n][...]
        qbuf[n, pl.ds(mine * g, mine)] = fresh[n][:, g]

    send_fresh(1)

    tok = q_ref.shape[0]
    tiles = tok // tile
    first_pos = lengths[me] + g * tok
    positions = first_pos + lax.broadcasted_iota(jnp.int32, (tok, half), 0)
    angles = positions.astype(jnp.float32) * freq[...]
    lane = lax.broadcasted_iota(jnp.int32, (tok, half), 1)
    cos_ref[...] = jnp.cos(angles)
    sin_all = jnp.sin(angles)
    sin_ref[...] = jnp.where(lane < quarter, -sin_all, sin_all)

    def turn(lead, trows):
        lead = lead.astype(jnp.float32)
        turned = pltpu.roll(lead, quarter, axis=1)
        return (lead * cos_ref[trows, :] + turned * sin_ref[trows, :]).astype(jnp.bfloat16)

    for t in range(tiles):
        trows = pl.ds(t * tile, tile)
        lead = new_k[t, :, :, :half].reshape(tile, half)
        fresh_k[t, :, :, :half] = turn(lead, trows).reshape(ng, rows, half)
        fresh_k[t, :, :, half:] = new_k[t, :, :, half:]
    get_q.wait()
    for t in range(tiles):
        trows = pl.ds(t * tile, tile)
        for h in range(heads):
            roped = turn(q_ref[trows, h * hd : h * hd + half], trows)
            qs[t, h * tile : (h + 1) * tile, :half] = roped * scale
            qs[t, h * tile : (h + 1) * tile, half:] = (
                q_ref[trows, h * hd + half : (h + 1) * hd] * scale
            )
    send_fresh(0)
    att = q_ref

    def block(q, dst):
        return pl.ds(mine * (q - dst), mine)

    def ag_near(n, q):
        return remote(
            comp.at[n, pl.ds(mine * q, mine)],
            windows[n].at[block(q, partner), g],
            s_ag.at[n, q, 0],
            r_ag.at[n, q, g],
            me,
            partner,
        )

    def ag_far(n, q, dst):
        return remote(
            comp.at[n, pl.ds(mine * q, mine)],
            windows[n].at[block(q, dst), g],
            s_ag.at[n, q, 1],
            r_ag.at[n, q, g],
            me,
            dst,
        )

    def ag_pass(n, q):
        return remote(
            windows[n].at[block(q, g), across],
            windows[n].at[block(q, partner), across],
            s_ag.at[n, q, 2],
            r_ag.at[n, q, across],
            me,
            partner,
        )

    def ag_from(n, q, src):
        return remote(
            comp.at[n, pl.ds(mine * q, mine)],
            windows[n].at[block(q, g), src],
            s_ag.at[n, q, 0],
            r_ag.at[n, q, src],
            me,
            partner,
        )

    def far_do(n, q, act):
        @pl.when(other + 1 <= q)
        def _():
            act(ag_far(n, q, across))

        @pl.when(other == q)
        def _():
            act(ag_far(n, q, other))

    def start(c):
        c.start()

    def sent(c):
        c.wait_send()

    for n in range(2):

        def wait_old(k, _):
            old_landed(n, k).wait_recv()
            return 0

        lax.fori_loop(1, nb, wait_old, 0)

        def pack(j, _):
            comp[n, j] = recv_old[n][table[me, j] // pages_here]
            return 0

        lax.fori_loop(0, old_pages, pack, 0)
        for q in range(ng):
            far_do(n, q, start)

            @pl.when(partner <= q)
            def _():
                ag_near(n, q).start()

            @pl.when(g <= q)
            def _():
                windows[n][block(q, g), g] = comp[n, pl.ds(mine * q, mine)]

        if n == 0:

            @pl.when(hi == 1)
            def _():
                for m in range(2):
                    fresh_from(m, across).wait_recv()
                    fresh_pass(m).start()

    @pl.when(core == 1)
    def _():
        for n in range(2):
            fresh_from(n, partner).wait_recv()

    @pl.when(hi == 1)
    def _():
        for n in range(2):
            fresh_from(n, 1 - core).wait_recv()

    for src in range(ng):

        @pl.when(src < g)
        def _():
            for n in range(2):
                qbuf[n, pl.ds(mine * src, mine)] = windows[n][fresh_at(src, g), g]

        @pl.when(src > g)
        def _():
            for n in range(2):
                quarter_from(n, src).wait_recv()

    def fill_new(a, _):
        i = tab[nb + a]
        send_new[a, 0] = qbuf[0, i]
        send_new[a, 1] = qbuf[1, i]
        return 0

    lax.fori_loop(0, nb, fill_new, 0)

    def new_copy(k):
        a = lax.rem(me + k, nb)
        return remote(send_new.at[a], newrecv.at[me], s_new.at[a], r_new.at[me], a, g)

    def new_landed(k):
        a = lax.rem(me + nb - k, nb)
        return remote(send_new.at[a], newrecv.at[a], s_new.at[a], r_new.at[a], a, g)

    def start_new(k, _):
        new_copy(k).start()
        return 0

    newrecv[me] = send_new[me]

    for n in range(2):
        for q in range(ng):

            @pl.when(2 * hi + 1 <= q)
            def _():
                ag_from(n, q, across).wait_recv()
                ag_pass(n, q).start()

    for n in range(2):
        for q in range(ng):

            @pl.when(g <= q)
            def _():
                ag_from(n, q, partner).wait_recv()
                ag_from(n, q, other + 1 - core).wait_recv()

            @pl.when(2 * hi == q)
            def _():
                @pl.when(core == 0)
                def _():
                    ag_from(n, q, across).wait_recv()

    lax.fori_loop(1, nb, start_new, 0)

    parts = 5
    stack = heads // parts
    high = stack * tile
    span = old_pages + 1
    keys = span * tile
    empty = lengths[me] <= 0
    blank = [jnp.logical_and(empty, k + g < ng) for k in range(ng)]
    score = (score0, score1)
    prob = (prob0, prob1)
    sums = (sums0, sums1)
    r = lax.broadcasted_iota(jnp.int32, (tile, tile), 0)
    c = lax.broadcasted_iota(jnp.int32, (tile, tile), 1)
    after, upto = c > r, c <= r

    def scores(t, part, slot):
        score[slot][...] = lax.dot_general(
            qs[t, part * high : (part + 1) * high, :],
            kbuf[t : t + span].reshape(keys, hd),
            (((1,), (1,)), ((), ())),
            preferred_element_type=jnp.float32,
        )

    def softmax(t, part, slot):
        for h in range(stack):
            hrows = slice(h * tile, (h + 1) * tile)
            runs = []
            for k in range(ng + 1):
                begin, end = max(mine * k, t) - t, min(mine * (k + 1) - t, span)
                runs.append(
                    [score[slot][hrows, p * tile : (p + 1) * tile] for p in range(begin, end)]
                )
            runs[0][0] = jnp.where(after, runs[0][0], NEG)
            runs[-1][-1] = jnp.where(upto, runs[-1][-1], NEG)
            tops = [functools.reduce(jnp.maximum, run) for run in runs]
            for k in range(ng):
                tops[k] = jnp.where(blank[k], NEG, tops[k])
            m = jnp.max(functools.reduce(jnp.maximum, tops), axis=1, keepdims=True)
            p = total = 0
            for k, run in enumerate(runs):
                mk = jnp.where(blank[k], -NEG, m) if k < ng else m
                for x in run:
                    e = jnp.exp(x - mk)
                    total = total + e
                    prob[slot][hrows, p * tile : (p + 1) * tile] = e.astype(jnp.bfloat16)
                    p += 1
            sums[slot][hrows, :] = jnp.broadcast_to(
                jnp.sum(total, axis=1, keepdims=True), (tile, tile)
            )
        o = jnp.dot(
            prob[slot][...],
            vbuf[t : t + span].reshape(keys, hd),
            preferred_element_type=jnp.float32,
        )
        o = (o / sums[slot][:, :1]).astype(jnp.bfloat16)
        for h in range(stack):
            col = (part * stack + h) * hd
            att[t * tile : (t + 1) * tile, col : col + hd] = o[h * tile : (h + 1) * tile]

    steps = [(t, part) for t in range(tiles) for part in range(parts)]
    scores(*steps[0], 0)
    for i, at in enumerate(steps):
        if i + 1 < len(steps):
            scores(*steps[i + 1], (i + 1) % 2)
        softmax(*at, i % 2)

    def put(n):
        cols = pl.ds(pl.multiple_of(n * wide, wide), wide)
        return pltpu.make_async_copy(hid.at[lax.rem(n, 2)], hidden.at[:, cols], out_sem.at[n])

    def project(n, _):
        get_w(n).wait()

        @pl.when(n >= 2)
        def _():
            put(n - 2).wait()

        hid[lax.rem(n, 2)] = jnp.dot(
            att[...], wbuf[lax.rem(n, slots)], preferred_element_type=jnp.float32
        ).astype(jnp.bfloat16)
        put(n).start()

        @pl.when(n + slots < chunks)
        def _():
            get_w(n + slots).start()

        return 0

    lax.fori_loop(0, chunks - 1, project, 0)

    def wait_new(k, _):
        new_landed(k).wait_recv()
        return 0

    lax.fori_loop(1, nb, wait_new, 0)

    def update(p, _):
        b = tab[2 * nb + p] - 1
        for n in range(2):
            arrived = newrecv[jnp.maximum(b, 0), n]
            pages[n, p] = jnp.where(b >= 0, arrived, caches[n][p])
        return 0

    lax.fori_loop(0, pages_here, update, 0)
    outs = [
        pltpu.make_async_copy(pages.at[n], dst, loc.at[2 + n])
        for n, dst in enumerate((key_out, value_out))
    ]
    for x in outs:
        x.start()
    project(jnp.int32(chunks - 1), 0)

    def wait_rest(k, _):
        old_copy(0, k).wait_send()
        old_copy(1, k).wait_send()
        new_copy(k).wait_send()
        return 0

    lax.fori_loop(1, nb, wait_rest, 0)

    @pl.when(hi == 0)
    def _():
        for n in range(2):
            fresh_far(n).wait_send()

    @pl.when(core == 0)
    def _():
        for n in range(2):
            fresh_near(n).wait_send()

    @pl.when(hi == 1)
    def _():
        for n in range(2):
            fresh_pass(n).wait_send()

    for n in range(2):
        for d in range(ng - 1):

            @pl.when(g > d)
            def _():
                quarter_to(n, d).wait_send()

        for q in range(ng):
            far_do(n, q, sent)

            @pl.when(partner <= q)
            def _():
                ag_near(n, q).wait_send()

            @pl.when(2 * hi + 1 <= q)
            def _():
                ag_pass(n, q).wait_send()

    for n in range(chunks - 2, chunks):
        put(n).wait()
    for x in outs:
        x.wait()


def body(queries, new_keys, new_values, key_cache, value_cache, out_weight, lengths, page_table):
    nb = lax.axis_size("blk")
    ng = lax.axis_size("group")
    me = lax.axis_index("blk")
    tok = queries.shape[1]
    hd = new_keys.shape[2]
    heads = queries.shape[2] // hd
    pages_here, rows = key_cache.shape[:2]
    slots = page_table.shape[1]
    fresh = tok // rows
    old = slots - fresh
    mine = fresh // ng
    bf16 = jnp.bfloat16

    quarter = hd // 4
    freq = 10000.0 ** (-jnp.arange(quarter, dtype=jnp.float32) / quarter)
    freq = jnp.concatenate([freq, freq])[None]

    i32 = jnp.int32
    at = jnp.arange(2 * nb + pages_here, dtype=i32)[:, None, None]
    b = jnp.arange(nb, dtype=i32)[None, :, None]
    j = jnp.arange(slots, dtype=i32)[None, None, :]
    own, local = (page_table // pages_here)[None], (page_table % pages_here)[None]
    wants = (at == b) & (j < old) & (own == me)
    gives = (at >= nb) & (at < 2 * nb) & (b == me) & (j >= old) & (own == at - nb)
    takes = (j >= old) & (own == me) & (local == at - 2 * nb)
    tab = jnp.sum(
        jnp.where(wants, local, jnp.where(gives, j - old, jnp.where(takes, b + 1, 0))), axis=(1, 2)
    )

    shape4 = (mine, ng, rows, hd)
    tile = rows * ng
    keys = (old + 1) * tile
    width = heads * hd
    dma = pltpu.SemaphoreType.DMA
    vmem = pltpu.VMEM
    hidden, key_out, value_out = pl.pallas_call(
        functools.partial(layer_kernel, (nb, ng, old, mine, heads, hd, hd**-0.5)),
        out_shape=(
            jax.ShapeDtypeStruct((tok, out_weight.shape[1]), bf16),
            jax.ShapeDtypeStruct(key_cache.shape, bf16),
            jax.ShapeDtypeStruct(value_cache.shape, bf16),
        ),
        in_specs=[SM, SM, SM, VM, VM, VM, VM, VM, ANY, ANY],
        out_specs=(ANY, ANY, ANY),
        scratch_shapes=[
            vmem(shape4, bf16),
            vmem((tok, hd // 2), jnp.float32),
            vmem((tok, hd // 2), jnp.float32),
            vmem((tok, width), bf16),
            vmem((3, width, out_weight.shape[1] // 5), bf16),
            vmem((tok // tile, heads * tile, hd), bf16),
            vmem((2, tok, out_weight.shape[1] // 5), bf16),
            vmem((2, *key_cache.shape), bf16),
            vmem((nb, 2, rows, hd), bf16),
            vmem((old + mine, ng, rows, hd), bf16),
            vmem((old + mine, ng, rows, hd), bf16),
            vmem((2, nb, rows, hd), bf16),
            vmem((nb, rows, hd), bf16),
            vmem((nb, rows, hd), bf16),
            vmem((2, old, rows, hd), bf16),
            vmem((2, fresh, rows, hd), bf16),
            vmem((nb, 2, rows, hd), bf16),
            vmem((heads // 5 * tile, keys), jnp.float32),
            vmem((heads // 5 * tile, keys), jnp.float32),
            vmem((heads // 5 * tile, keys), bf16),
            vmem((heads // 5 * tile, keys), bf16),
            vmem((heads // 5 * tile, tile), jnp.float32),
            vmem((heads // 5 * tile, tile), jnp.float32),
            dma((2, nb)),
            dma((2, nb)),
            dma((2, 3)),
            dma((2, ng)),
            dma((2, ng)),
            dma((2, ng)),
            dma((2, ng, 3)),
            dma((2, ng, ng)),
            dma((nb,)),
            dma((nb,)),
            dma((4,)),
            dma((5,)),
            dma((3,)),
        ],
        compiler_params=pltpu.CompilerParams(
            collective_id=0, has_side_effects=True, vmem_limit_bytes=67_043_328
        ),
        name="layer",
    )(
        tab,
        page_table,
        lengths,
        freq,
        new_keys[0].reshape(shape4),
        new_values[0].reshape(shape4),
        key_cache,
        value_cache,
        queries[0],
        out_weight,
    )
    return (hidden[None], key_out, value_out)


def solution(mesh):
    split = P("blk", "group", None)
    return jax.shard_map(
        body,
        mesh=mesh,
        in_specs=(split, split, split, split, split, P(), P(), P()),
        out_specs=(split, split, split),
        check_vma=False,
    )
```

```python
import functools

import jax
import jax.numpy as jnp
from jax import lax
from jax.experimental import pallas as pl
from jax.experimental.pallas import tpu as pltpu
from jax.sharding import PartitionSpec as P

MESH = pl.DeviceIdType.MESH
NEG = -1e30
ANY = pl.BlockSpec(memory_space=pl.ANY)
VM = pl.BlockSpec(memory_space=pltpu.VMEM)
SM = pl.BlockSpec(memory_space=pltpu.SMEM)


def layer_kernel(
    dims,
    tab,
    table,
    lengths,
    freq,
    new_k,
    fresh_v,
    kcache,
    vcache,
    queries,
    weight,
    hidden,
    key_out,
    value_out,
    fresh_k,
    cos_ref,
    sin_ref,
    q_ref,
    wbuf,
    qs,
    hid,
    pages,
    newrecv,
    kbuf,
    vbuf,
    send_old,
    recv_k,
    recv_v,
    comp,
    qbuf,
    send_new,
    score0,
    score1,
    prob0,
    prob1,
    sums0,
    sums1,
    s_old,
    r_old,
    s_fr,
    r_fr,
    s_q,
    r_q,
    s_ag,
    r_ag,
    s_new,
    r_new,
    loc,
    out_sem,
    w_sem,
):
    nb, ng, old_pages, mine, heads, hd, scale = dims
    pages_here = kcache.shape[0]
    me = lax.axis_index("blk")
    g = lax.axis_index("group")
    core = lax.rem(g, 2)
    hi = g // 2
    partner = 2 * hi + 1 - core
    across = 2 * (1 - hi) + core
    other = 2 * (1 - hi)
    windows = (kbuf, vbuf)
    fresh = (fresh_k, fresh_v)
    caches = (kcache, vcache)
    recv_old = (recv_k, recv_v)
    rows = kcache.shape[1]
    tile = rows * ng
    half = hd // 2
    quarter = half // 2

    def remote(src, dst, ssem, rsem, blk, grp):
        return pltpu.make_async_remote_copy(
            src_ref=src,
            dst_ref=dst,
            send_sem=ssem,
            recv_sem=rsem,
            device_id={"blk": blk, "group": grp},
            device_id_type=MESH,
        )

    get_q = pltpu.make_async_copy(queries, q_ref, loc.at[0])
    get_q.start()
    chunks = 5
    slots = wbuf.shape[0]
    wide = wbuf.shape[2]

    def get_w(n):
        cols = pl.ds(pl.multiple_of(n * wide, wide), wide)
        return pltpu.make_async_copy(
            weight.at[:, cols], wbuf.at[lax.rem(n, slots)], w_sem.at[lax.rem(n, slots)]
        )

    for n in range(slots):
        get_w(jnp.int32(n)).start()

    barrier = pltpu.get_barrier_semaphore()

    def greet(k, _):
        pl.semaphore_signal(
            barrier, inc=1, device_id={"blk": lax.rem(me + k, nb), "group": g}, device_id_type=MESH
        )
        return 0

    lax.fori_loop(1, nb, greet, 0)
    for d in range(1, ng):
        pl.semaphore_signal(
            barrier, inc=1, device_id={"blk": me, "group": lax.rem(g + d, ng)}, device_id_type=MESH
        )

    for n in range(2):

        def fill(a, _):
            send_old[n, a] = caches[n][tab[a]]
            return 0

        lax.fori_loop(0, nb, fill, 0)
        recv_old[n][me] = send_old[n, me]
    pl.semaphore_wait(barrier, nb - 1 + ng - 1)

    def old_copy(n, k):
        a = lax.rem(me + k, nb)
        return remote(
            send_old.at[n, a], recv_old[n].at[me], s_old.at[n, a], r_old.at[n, me], a, g
        )

    def old_landed(n, k):
        a = lax.rem(me + nb - k, nb)
        return remote(send_old.at[n, a], recv_old[n].at[a], s_old.at[n, a], r_old.at[n, a], a, g)

    for n in range(2):

        def start_old(k, _):
            old_copy(n, k).start()
            return 0

        lax.fori_loop(1, nb, start_old, 0)

    def fresh_at(src, dst):
        return pl.ds(old_pages + mine * (src - dst), mine)

    def fresh_near(n):
        return remote(
            fresh[n], windows[n].at[fresh_at(g, partner)], s_fr.at[n, 0], r_fr.at[n, g], me, partner
        )

    def fresh_far(n):
        return remote(
            fresh[n], windows[n].at[fresh_at(g, across)], s_fr.at[n, 1], r_fr.at[n, g], me, across
        )

    def fresh_pass(n):
        return remote(
            windows[n].at[fresh_at(across, g)],
            windows[n].at[fresh_at(across, partner)],
            s_fr.at[n, 2],
            r_fr.at[n, across],
            me,
            partner,
        )

    def fresh_from(n, src):
        return remote(
            fresh[n], windows[n].at[fresh_at(src, g)], s_fr.at[n, 0], r_fr.at[n, src], me, partner
        )

    def quarter_to(n, dst):
        return remote(
            fresh[n].at[:, dst],
            qbuf.at[n, pl.ds(mine * g, mine)],
            s_q.at[n, dst],
            r_q.at[n, g],
            me,
            dst,
        )

    def quarter_from(n, src):
        return remote(
            fresh[n].at[:, g],
            qbuf.at[n, pl.ds(mine * src, mine)],
            s_q.at[n, g],
            r_q.at[n, src],
            me,
            partner,
        )

    def send_fresh(n):
        @pl.when(hi == 0)
        def _():
            fresh_far(n).start()

        @pl.when(core == 0)
        def _():
            fresh_near(n).start()

        for d in range(ng - 1):

            @pl.when(g > d)
            def _():
                quarter_to(n, d).start()

        windows[n][pl.ds(old_pages, mine)] = fresh[n][...]
        qbuf[n, pl.ds(mine * g, mine)] = fresh[n][:, g]

    tok = q_ref.shape[0]
    tiles = tok // tile
    first_pos = lengths[me] + g * tok
    positions = first_pos + lax.broadcasted_iota(jnp.int32, (tok, half), 0)
    angles = positions.astype(jnp.float32) * freq[...]
    lane = lax.broadcasted_iota(jnp.int32, (tok, half), 1)
    cos_ref[...] = jnp.cos(angles)
    sin_all = jnp.sin(angles)
    sin_ref[...] = jnp.where(lane < quarter, -sin_all, sin_all)

    def turn(lead, trows):
        lead = lead.astype(jnp.float32)
        turned = pltpu.roll(lead, quarter, axis=1)
        return (lead * cos_ref[trows, :] + turned * sin_ref[trows, :]).astype(jnp.bfloat16)

    for t in range(tiles):
        trows = pl.ds(t * tile, tile)
        lead = new_k[t, :, :, :half].reshape(tile, half)
        fresh_k[t, :, :, :half] = turn(lead, trows).reshape(ng, rows, half)
        fresh_k[t, :, :, half:] = new_k[t, :, :, half:]
    get_q.wait()
    for t in range(tiles):
        trows = pl.ds(t * tile, tile)
        for h in range(heads):
            roped = turn(q_ref[trows, h * hd : h * hd + half], trows)
            qs[t, h * tile : (h + 1) * tile, :half] = roped * scale
            qs[t, h * tile : (h + 1) * tile, half:] = (
                q_ref[trows, h * hd + half : (h + 1) * hd] * scale
            )
    att = q_ref

    def block(q, dst):
        return pl.ds(mine * (q - dst), mine)

    def ag_near(n, q):
        return remote(
            comp.at[n, pl.ds(mine * q, mine)],
            windows[n].at[block(q, partner), g],
            s_ag.at[n, q, 0],
            r_ag.at[n, q, g],
            me,
            partner,
        )

    def ag_far(n, q, dst):
        return remote(
            comp.at[n, pl.ds(mine * q, mine)],
            windows[n].at[block(q, dst), g],
            s_ag.at[n, q, 1],
            r_ag.at[n, q, g],
            me,
            dst,
        )

    def ag_pass(n, q):
        return remote(
            windows[n].at[block(q, g), across],
            windows[n].at[block(q, partner), across],
            s_ag.at[n, q, 2],
            r_ag.at[n, q, across],
            me,
            partner,
        )

    def ag_from(n, q, src):
        return remote(
            comp.at[n, pl.ds(mine * q, mine)],
            windows[n].at[block(q, g), src],
            s_ag.at[n, q, 0],
            r_ag.at[n, q, src],
            me,
            partner,
        )

    def far_do(n, q, act):
        @pl.when(other + 1 <= q)
        def _():
            act(ag_far(n, q, across))

        @pl.when(other == q)
        def _():
            act(ag_far(n, q, other))

    def start(c):
        c.start()

    def sent(c):
        c.wait_send()

    for n in range(2):

        def wait_old(k, _):
            old_landed(n, k).wait_recv()
            return 0

        lax.fori_loop(1, nb, wait_old, 0)

        def pack(j, _):
            comp[n, j] = recv_old[n][table[me, j] // pages_here]
            return 0

        lax.fori_loop(0, old_pages, pack, 0)
        for q in range(ng):
            far_do(n, q, start)

            @pl.when(partner <= q)
            def _():
                ag_near(n, q).start()

            @pl.when(g <= q)
            def _():
                windows[n][block(q, g), g] = comp[n, pl.ds(mine * q, mine)]

        if n == 0:
            send_fresh(0)
            send_fresh(1)

    @pl.when(hi == 1)
    def _():
        for m in range(2):
            fresh_from(m, across).wait_recv()
            fresh_pass(m).start()

    @pl.when(core == 1)
    def _():
        for n in range(2):
            fresh_from(n, partner).wait_recv()

    @pl.when(hi == 1)
    def _():
        for n in range(2):
            fresh_from(n, 1 - core).wait_recv()

    for src in range(ng):

        @pl.when(src < g)
        def _():
            for n in range(2):
                qbuf[n, pl.ds(mine * src, mine)] = windows[n][fresh_at(src, g), g]

        @pl.when(src > g)
        def _():
            for n in range(2):
                quarter_from(n, src).wait_recv()

    def fill_new(a, _):
        i = tab[nb + a]
        send_new[a, 0] = qbuf[0, i]
        send_new[a, 1] = qbuf[1, i]
        return 0

    lax.fori_loop(0, nb, fill_new, 0)

    def new_copy(k):
        a = lax.rem(me + k, nb)
        return remote(send_new.at[a], newrecv.at[me], s_new.at[a], r_new.at[me], a, g)

    def new_landed(k):
        a = lax.rem(me + nb - k, nb)
        return remote(send_new.at[a], newrecv.at[a], s_new.at[a], r_new.at[a], a, g)

    def start_new(k, _):
        new_copy(k).start()
        return 0

    newrecv[me] = send_new[me]

    for n in range(2):
        for q in range(ng):

            @pl.when(2 * hi + 1 <= q)
            def _():
                ag_from(n, q, across).wait_recv()
                ag_pass(n, q).start()

    for n in range(2):
        for q in range(ng):

            @pl.when(g <= q)
            def _():
                ag_from(n, q, partner).wait_recv()
                ag_from(n, q, other + 1 - core).wait_recv()

            @pl.when(2 * hi == q)
            def _():
                @pl.when(core == 0)
                def _():
                    ag_from(n, q, across).wait_recv()

    lax.fori_loop(1, nb, start_new, 0)

    parts = 5
    stack = heads // parts
    high = stack * tile
    span = old_pages + 1
    keys = span * tile
    empty = lengths[me] <= 0
    blank = [jnp.logical_and(empty, k + g < ng) for k in range(ng)]
    score = (score0, score1)
    prob = (prob0, prob1)
    sums = (sums0, sums1)
    r = lax.broadcasted_iota(jnp.int32, (tile, tile), 0)
    c = lax.broadcasted_iota(jnp.int32, (tile, tile), 1)
    after, upto = c > r, c <= r

    def scores(t, part, slot):
        score[slot][...] = lax.dot_general(
            qs[t, part * high : (part + 1) * high, :],
            kbuf[t : t + span].reshape(keys, hd),
            (((1,), (1,)), ((), ())),
            preferred_element_type=jnp.float32,
        )

    def softmax(t, part, slot):
        for h in range(stack):
            hrows = slice(h * tile, (h + 1) * tile)
            runs = []
            for k in range(ng + 1):
                begin, end = max(mine * k, t) - t, min(mine * (k + 1) - t, span)
                runs.append(
                    [score[slot][hrows, p * tile : (p + 1) * tile] for p in range(begin, end)]
                )
            runs[0][0] = jnp.where(after, runs[0][0], NEG)
            runs[-1][-1] = jnp.where(upto, runs[-1][-1], NEG)
            tops = [functools.reduce(jnp.maximum, run) for run in runs]
            for k in range(ng):
                tops[k] = jnp.where(blank[k], NEG, tops[k])
            m = jnp.max(functools.reduce(jnp.maximum, tops), axis=1, keepdims=True)
            p = total = 0
            for k, run in enumerate(runs):
                mk = jnp.where(blank[k], -NEG, m) if k < ng else m
                for x in run:
                    e = jnp.exp(x - mk)
                    total = total + e
                    prob[slot][hrows, p * tile : (p + 1) * tile] = e.astype(jnp.bfloat16)
                    p += 1
            sums[slot][hrows, :] = jnp.broadcast_to(
                jnp.sum(total, axis=1, keepdims=True), (tile, tile)
            )
        o = jnp.dot(
            prob[slot][...],
            vbuf[t : t + span].reshape(keys, hd),
            preferred_element_type=jnp.float32,
        )
        o = (o / sums[slot][:, :1]).astype(jnp.bfloat16)
        for h in range(stack):
            col = (part * stack + h) * hd
            att[t * tile : (t + 1) * tile, col : col + hd] = o[h * tile : (h + 1) * tile]

    steps = [(t, part) for t in range(tiles) for part in range(parts)]
    scores(*steps[0], 0)
    for i, at in enumerate(steps):
        if i + 1 < len(steps):
            scores(*steps[i + 1], (i + 1) % 2)
        softmax(*at, i % 2)

    def put(n):
        cols = pl.ds(pl.multiple_of(n * wide, wide), wide)
        return pltpu.make_async_copy(hid.at[lax.rem(n, 2)], hidden.at[:, cols], out_sem.at[n])

    def project(n, _):
        get_w(n).wait()

        @pl.when(n >= 2)
        def _():
            put(n - 2).wait()

        hid[lax.rem(n, 2)] = jnp.dot(
            att[...], wbuf[lax.rem(n, slots)], preferred_element_type=jnp.float32
        ).astype(jnp.bfloat16)
        put(n).start()

        @pl.when(n + slots < chunks)
        def _():
            get_w(n + slots).start()

        return 0

    lax.fori_loop(0, chunks - 1, project, 0)

    def wait_new(k, _):
        new_landed(k).wait_recv()
        return 0

    lax.fori_loop(1, nb, wait_new, 0)

    def update(p, _):
        b = tab[2 * nb + p] - 1
        for n in range(2):
            arrived = newrecv[jnp.maximum(b, 0), n]
            pages[n, p] = jnp.where(b >= 0, arrived, caches[n][p])
        return 0

    lax.fori_loop(0, pages_here, update, 0)
    outs = [
        pltpu.make_async_copy(pages.at[n], dst, loc.at[2 + n])
        for n, dst in enumerate((key_out, value_out))
    ]
    for x in outs:
        x.start()
    project(jnp.int32(chunks - 1), 0)

    def wait_rest(k, _):
        old_copy(0, k).wait_send()
        old_copy(1, k).wait_send()
        new_copy(k).wait_send()
        return 0

    lax.fori_loop(1, nb, wait_rest, 0)

    @pl.when(hi == 0)
    def _():
        for n in range(2):
            fresh_far(n).wait_send()

    @pl.when(core == 0)
    def _():
        for n in range(2):
            fresh_near(n).wait_send()

    @pl.when(hi == 1)
    def _():
        for n in range(2):
            fresh_pass(n).wait_send()

    for n in range(2):
        for d in range(ng - 1):

            @pl.when(g > d)
            def _():
                quarter_to(n, d).wait_send()

        for q in range(ng):
            far_do(n, q, sent)

            @pl.when(partner <= q)
            def _():
                ag_near(n, q).wait_send()

            @pl.when(2 * hi + 1 <= q)
            def _():
                ag_pass(n, q).wait_send()

    for n in range(chunks - 2, chunks):
        put(n).wait()
    for x in outs:
        x.wait()


def settle_kernel(parts, *refs):
    n = len(refs) // 3
    given, wanted, held = refs[:n], refs[n : 2 * n], refs[2 * n : 3 * n]
    sem = refs[-1]
    moves = []
    for src, dst, buf, cuts in zip(given, wanted, held, parts):
        size = src.shape[0] // cuts
        for i in range(cuts):
            at = pl.ds(i * size, size)
            k = len(moves)
            moves.append(
                (
                    pltpu.make_async_copy(src.at[at], buf.at[at], sem.at[0, k]),
                    pltpu.make_async_copy(buf.at[at], dst.at[at], sem.at[1, k]),
                )
            )
    for take, _ in moves:
        take.start()
    for take, give in moves:
        take.wait()
        give.start()
    for _, give in moves:
        give.wait()


def body(queries, new_keys, new_values, key_cache, value_cache, out_weight, lengths, page_table):
    nb = lax.axis_size("blk")
    ng = lax.axis_size("group")
    me = lax.axis_index("blk")
    tok = queries.shape[1]
    hd = new_keys.shape[2]
    heads = queries.shape[2] // hd
    pages_here, rows = key_cache.shape[:2]
    slots = page_table.shape[1]
    fresh = tok // rows
    old = slots - fresh
    mine = fresh // ng
    bf16 = jnp.bfloat16

    quarter = hd // 4
    freq = 10000.0 ** (-jnp.arange(quarter, dtype=jnp.float32) / quarter)
    freq = jnp.concatenate([freq, freq])[None]

    i32 = jnp.int32
    at = jnp.arange(2 * nb + pages_here, dtype=i32)[:, None, None]
    b = jnp.arange(nb, dtype=i32)[None, :, None]
    j = jnp.arange(slots, dtype=i32)[None, None, :]
    own, local = (page_table // pages_here)[None], (page_table % pages_here)[None]
    wants = (at == b) & (j < old) & (own == me)
    gives = (at >= nb) & (at < 2 * nb) & (b == me) & (j >= old) & (own == at - nb)
    takes = (j >= old) & (own == me) & (local == at - 2 * nb)
    tab = jnp.sum(
        jnp.where(wants, local, jnp.where(gives, j - old, jnp.where(takes, b + 1, 0))), axis=(1, 2)
    )

    shape4 = (mine, ng, rows, hd)
    tile = rows * ng
    keys = (old + 1) * tile
    width = heads * hd
    dma = pltpu.SemaphoreType.DMA
    vmem = pltpu.VMEM
    hidden, key_out, value_out = pl.pallas_call(
        functools.partial(layer_kernel, (nb, ng, old, mine, heads, hd, hd**-0.5)),
        out_shape=(
            jax.ShapeDtypeStruct((tok, out_weight.shape[1]), bf16),
            jax.ShapeDtypeStruct(key_cache.shape, bf16),
            jax.ShapeDtypeStruct(value_cache.shape, bf16),
        ),
        in_specs=[SM, SM, SM, VM, VM, VM, VM, VM, ANY, ANY],
        out_specs=(ANY, ANY, ANY),
        scratch_shapes=[
            vmem(shape4, bf16),
            vmem((tok, hd // 2), jnp.float32),
            vmem((tok, hd // 2), jnp.float32),
            vmem((tok, width), bf16),
            vmem((3, width, out_weight.shape[1] // 5), bf16),
            vmem((tok // tile, heads * tile, hd), bf16),
            vmem((2, tok, out_weight.shape[1] // 5), bf16),
            vmem((2, *key_cache.shape), bf16),
            vmem((nb, 2, rows, hd), bf16),
            vmem((old + mine, ng, rows, hd), bf16),
            vmem((old + mine, ng, rows, hd), bf16),
            vmem((2, nb, rows, hd), bf16),
            vmem((nb, rows, hd), bf16),
            vmem((nb, rows, hd), bf16),
            vmem((2, old, rows, hd), bf16),
            vmem((2, fresh, rows, hd), bf16),
            vmem((nb, 2, rows, hd), bf16),
            vmem((heads // 5 * tile, keys), jnp.float32),
            vmem((heads // 5 * tile, keys), jnp.float32),
            vmem((heads // 5 * tile, keys), bf16),
            vmem((heads // 5 * tile, keys), bf16),
            vmem((heads // 5 * tile, tile), jnp.float32),
            vmem((heads // 5 * tile, tile), jnp.float32),
            dma((2, nb)),
            dma((2, nb)),
            dma((2, 3)),
            dma((2, ng)),
            dma((2, ng)),
            dma((2, ng)),
            dma((2, ng, 3)),
            dma((2, ng, ng)),
            dma((nb,)),
            dma((nb,)),
            dma((4,)),
            dma((5,)),
            dma((3,)),
        ],
        compiler_params=pltpu.CompilerParams(
            collective_id=0, has_side_effects=True, vmem_limit_bytes=67_043_328
        ),
        name="layer",
    )(
        tab,
        page_table,
        lengths,
        freq,
        new_keys[0].reshape(shape4),
        new_values[0].reshape(shape4),
        key_cache,
        value_cache,
        queries[0],
        out_weight,
    )
    results = (hidden, key_out, value_out)
    parts = (8, 2, 2)
    hidden, key_out, value_out = pl.pallas_call(
        functools.partial(settle_kernel, parts),
        out_shape=tuple(jax.ShapeDtypeStruct(x.shape, x.dtype) for x in results),
        in_specs=[ANY] * 3,
        out_specs=(ANY,) * 3,
        scratch_shapes=[*(vmem(x.shape, x.dtype) for x in results), dma((2, sum(parts)))],
        name="settle",
    )(*results)
    return (hidden[None], key_out, value_out)


def solution(mesh):
    split = P("blk", "group", None)
    return jax.shard_map(
        body,
        mesh=mesh,
        in_specs=(split, split, split, split, split, P(), P(), P()),
        out_specs=(split, split, split),
        check_vma=False,
    )
```
